512 devices in a mesh: group: 16 (over z, y_hi), rep: 32 (over x, y_lo, core).
Axes of the slice: x: 4, y: 8 (y_hi: 2, y_lo: 4; y = y_hi * 4 + y_lo), z: 8, core: 2. Of those that a mesh axis runs over, the one named last changes fastest.
Arguments:
- tokens: bfloat16 [16, 8192, 2048], P('group', 'rep'), may hold values from -6 to 6
- cotangent: bfloat16 [16, 8192, 4096], P('group', 'rep'), may hold values from -6 to 6
- gate_weight: float32 [16, 32, 256, 128], P('group', 'rep'), may hold values from -5 to 5
- up_weight: float32 [16, 32, 256, 128], P('group', 'rep'), may hold values from -5 to 5
- tile_rows: int32 [32, 2], replicated, may hold values from 0 to 15, as said below
- step: int32 [1], replicated, may hold values from 0 to 999
Outputs:
- new_gate: float32 [16, 32, 256, 128], P('group', 'rep')
The draws below stay inside these ranges and needn't reach their ends.
Inputs may be any that keep to these rules, and one draw needn't show every extreme that they name: `tile_rows`: the 2 entries of a row are distinct, and every feature block is named by some row.
All inputs are finite; a program needn't handle non-finite values.
Results may differ from the reference program's by a relative error of at most 0.0024.
Values may be sent and summed in bfloat16 or wider, within the bound.
No kernel may reach another device: no remote copies, remote signals or barrier semaphores. Data moves between devices by JAX's collectives and lax.ppermute only.
A program may use at most 64 MiB of HBM per device.

```python
import jax
import jax.numpy as jnp
from jax import lax

D = 2048
FFW = 4096
TILE = 128
PER_COL = 2
TOK_DEV = 256
DT = 16
FT = 32
TOKG = 8192
N_GROUP = 16
N_REP = 32


def draw_tile_rows(key, part):
    first_key = jax.random.fold_in(key, 11)
    second_key = jax.random.fold_in(key, 23)
    shuffled = jax.random.permutation(first_key, DT).astype(jnp.int32)
    first_rows = jnp.take(shuffled, jnp.arange(FT, dtype=jnp.int32) % DT)
    offsets = jax.random.randint(second_key, (FT,), 1, DT).astype(jnp.int32)
    second_rows = (first_rows + offsets) % DT
    return jnp.stack([first_rows, second_rows], 1).astype(jnp.int32)


def raised(values, key, source, target, parts, factor):
    owner, partner = [(jnp.arange(values.shape[position]) // (values.shape[position] // parts)).reshape([-1 if axis == position else 1 for axis in range(values.ndim)]) for position in (source, target)]
    chosen = jax.random.permutation(key, parts)[partner]
    strong = (owner == chosen) | (owner == (partner + parts // 2) % parts)
    return jnp.where(strong, factor * values, values)


def steps_of(stream_key, extent, shards, least, largest):
    factor_of, own = 1.0, jax.random.fold_in(stream_key, 6)
    for position, blocks in shards:
        draws = jnp.exp(jax.random.uniform(jax.random.fold_in(own, position), (blocks,), jnp.float32, least / len(shards), largest / len(shards)))
        factor_of = factor_of * jnp.repeat(draws, extent[position] // blocks).reshape([-1 if axis == position else 1 for axis in range(len(extent))])
    return factor_of


def centred(own_key, dims, deviation, most, split=(), kind=jnp.bfloat16):
    gain = steps_of(own_key, dims, split, -0.22, 0.18) if split else 1.0
    drawn = jax.random.normal(own_key, dims, jnp.float32) * deviation * gain
    return jnp.minimum(jnp.maximum(drawn, -most), most).astype(kind)


def noise_with(stream_key, dims, scale, most, cuts, heavy, kind=jnp.bfloat16):
    entries = scale * jax.random.normal(stream_key, dims, jnp.float32)
    if cuts:
        entries = entries * steps_of(stream_key, dims, cuts, -0.22, 0.18)
    return jnp.clip(raised(entries, jax.random.fold_in(stream_key, 3), *heavy), -most, most).astype(kind)


def setup_inputs(seed: int = 0) -> dict:
    keys = jax.random.split(jax.random.key(seed), 7)
    tokens = centred(keys[0], (N_GROUP, TOKG, D), 1.0, 6.0, ((0, 16), (1, 32)))
    cotangent = noise_with(keys[1], (N_GROUP, TOKG, FFW), 1.0, 6.0, ((0, 16), (1, 32)), (1, 2, 32, 2.75))
    gate_weight = centred(keys[2], (N_GROUP, FT, PER_COL * TILE, TILE), 1.0, 5.0, ((0, 16), (1, 32)), jnp.float32)
    up_weight = centred(keys[3], (N_GROUP, FT, PER_COL * TILE, TILE), 1.0, 5.0, ((0, 16), (1, 32)), jnp.float32)
    tile_rows = draw_tile_rows(jax.random.fold_in(keys[6], 71), 0)
    step = jax.random.randint(keys[5], (1,), 0, 1000).astype(jnp.int32)
    return {"tokens": tokens, "cotangent": cotangent, "gate_weight": gate_weight, "up_weight": up_weight, "tile_rows": tile_rows, "step": step}


LEARNING_RATE = 0.1


def reference(tokens, cotangent, gate_weight, up_weight, tile_rows, step):
    scaling = (PER_COL * TILE) ** -0.5

    def one_group(inputs_group):
        activ, cot_rows, gate_w, up_w = inputs_group
        weight_pair = jnp.concatenate([gate_w.astype(jnp.bfloat16), up_w.astype(jnp.bfloat16)], -1).astype(jnp.float32)
        activ_blocks = activ.reshape(N_REP, TOK_DEV, D // TILE, TILE)
        cot_blocks = cot_rows.reshape(N_REP, TOK_DEV, FFW // TILE, TILE)

        def accumulate(running, inputs_pair):
            rows_x, rows_c = inputs_pair
            selected = rows_x[:, tile_rows].reshape(TOK_DEV, FFW // TILE, PER_COL * TILE)
            combined = jnp.einsum('tfk,fke->tfe', selected.astype(jnp.float32), weight_pair) * scaling
            gate_vals = combined[..., :TILE]
            up_vals = combined[..., TILE:]
            sigmoid_gate = jax.nn.sigmoid(gate_vals)
            grad_gate = (rows_c * up_vals * sigmoid_gate * (1.0 + gate_vals * (1.0 - sigmoid_gate))).astype(jnp.bfloat16)
            part_sum = jnp.einsum('tfk,tfe->fke', selected.astype(jnp.float32), grad_gate.astype(jnp.float32)) * scaling
            return running + part_sum, None

        start_sum = jnp.zeros((FFW // TILE, PER_COL * TILE, TILE), jnp.float32)
        grad_total, _ = lax.scan(accumulate, start_sum, (activ_blocks, cot_blocks))
        return gate_w - LEARNING_RATE * grad_total

    stepped = lax.map(one_group, (tokens, cotangent, gate_weight, up_weight))
    levels = N_GROUP.bit_length() - 1
    chosen_bit = step[0] % levels
    partner_ids = jnp.bitwise_xor(jnp.arange(N_GROUP, dtype=jnp.int32), jnp.left_shift(jnp.int32(1), chosen_bit).astype(jnp.int32))
    return 0.5 * (stepped + stepped[partner_ids])
```

```python
from functools import partial

import jax
import jax.numpy as jnp
from jax import lax
from jax.experimental import pallas as pl
from jax.experimental.pallas import tpu as pltpu
from jax.sharding import PartitionSpec as P

TILE = 128
PER_COL = 2
LEARNING_RATE = 0.1
NX, NY, NC = 4, 4, 2


def place(x, y, c):
    return (x % NX) * NY * NC + (y % NY) * NC + c


PLACES = [(x, y, c) for x in range(NX) for y in range(NY) for c in range(NC)]
X_GROUPS = [[place(x, y, c) for x in range(NX)] for y in range(NY) for c in range(NC)]
Y_GROUPS = [[place(x, y, c) for y in range(NY)] for x in range(NX) for c in range(NC)]


def shift_x(value, by):
    return lax.ppermute(value, "rep", [(place(x, y, c), place(x + by, y, c)) for x, y, c in PLACES])


def swap_cores(value):
    return lax.ppermute(value, "rep", [(place(x, y, c), place(x, y, 1 - c)) for x, y, c in PLACES])


def partner(value, bit):
    return lax.ppermute(value, "group", [(i, i ^ 1 << bit) for i in range(lax.axis_size("group"))])


def grad_kernel(offsets, rows_ref, *refs):
    count = len(offsets)
    toks, cots = refs[0:2], refs[2:4]
    gates, ups = refs[4 : 4 + count], refs[4 + count : 4 + 2 * count]
    out_ref = refs[4 + 2 * count]
    scaling = (PER_COL * TILE) ** (-0.5)
    me = lax.axis_index("rep")
    my_x, core = me // (NY * NC), me % NC
    for number, offset in enumerate(offsets):
        column = lax.rem(my_x + offset, NX)

        def one(row, carry, number=number, column=column):
            hidden = column * (NY * NC) + row * NC + core
            weight = jnp.concatenate([gates[number][row], ups[number][row]], axis=-1)
            first = pl.multiple_of(rows_ref[hidden, 0] * TILE, TILE)
            second = pl.multiple_of(rows_ref[hidden, 1] * TILE, TILE)
            at = pl.multiple_of(hidden * TILE, TILE)
            total = None
            for tok, cot in zip(toks, cots):
                selected = jnp.concatenate([tok[:, pl.ds(first, TILE)], tok[:, pl.ds(second, TILE)]], axis=-1)
                both = jnp.dot(selected, weight, preferred_element_type=jnp.float32) * scaling
                gate, up = both[:, :TILE], both[:, TILE:]
                q = jax.nn.sigmoid(gate)
                grad = cot[:, pl.ds(at, TILE)].astype(jnp.float32) * up * q * (1.0 + gate * (1.0 - q))
                part = lax.dot_general(
                    selected,
                    grad.astype(jnp.bfloat16),
                    (((0,), (0,)), ((), ())),
                    preferred_element_type=jnp.float32,
                )
                total = part if total is None else total + part
            out_ref[column, row] = (total * scaling).astype(jnp.bfloat16)
            return carry

        lax.fori_loop(0, NY, one, 0, unroll=2)


def partial_sums(offsets, tile_rows, toks, cots, gates, ups):
    vmem = pl.BlockSpec(memory_space=pltpu.VMEM)
    return pl.pallas_call(
        partial(grad_kernel, offsets),
        out_shape=jax.ShapeDtypeStruct((NX, NY, PER_COL * TILE, TILE), jnp.bfloat16),
        in_specs=[pl.BlockSpec(memory_space=pltpu.SMEM)] + [vmem] * (4 + 2 * len(offsets)),
        out_specs=vmem,
        compiler_params=pltpu.CompilerParams(vmem_limit_bytes=48 * 1024 * 1024),
        name="partial_sums",
    )(tile_rows, *toks, *cots, *gates, *ups)


def body(tokens, cotangent, gate_weight, up_weight, tile_rows, step):
    tok, cot = tokens[0], cotangent[0]
    master = gate_weight[0, 0]
    gate_low = master.astype(jnp.bfloat16)
    up_low = up_weight[0, 0].astype(jnp.bfloat16)
    tok_peer, cot_peer = swap_cores(tok), swap_cores(cot)
    gate0 = lax.all_gather(gate_low, "rep", axis=0, axis_index_groups=Y_GROUPS)
    up0 = lax.all_gather(up_low, "rep", axis=0, axis_index_groups=Y_GROUPS)
    gate_l, up_r = shift_x(gate0, 1), shift_x(up0, -1)
    up_l, gate_r = shift_x(up0, 1), shift_x(gate0, -1)
    gate_o, up_o = shift_x(gate_l, 1), shift_x(up_r, -1)
    sums = partial_sums(
        (0, 3, 1, 2),
        tile_rows,
        (tok, tok_peer),
        (cot, cot_peer),
        (gate0, gate_l, gate_r, gate_o),
        (up0, up_l, up_r, up_o),
    )
    got = lax.all_to_all(sums, "rep", 0, 0, tiled=True, axis_index_groups=X_GROUPS)
    column = jnp.sum(got.astype(jnp.float32), axis=0).astype(jnp.bfloat16)
    got = lax.all_to_all(column, "rep", 0, 0, tiled=True, axis_index_groups=Y_GROUPS)
    total = jnp.sum(got.astype(jnp.float32), axis=0)
    stepped = master - LEARNING_RATE * total
    levels = lax.axis_size("group").bit_length() - 1
    branches = [partial(partner, bit=number) for number in range(levels)]
    other = lax.switch(step[0] % levels, branches, stepped)
    return (0.5 * (stepped + other))[None, None]


def solution(mesh):
    placed = (
        P("group", "rep", None),
        P("group", "rep", None),
        P("group", "rep", None, None),
        P("group", "rep", None, None),
        P(),
        P(),
    )
    return jax.shard_map(
        body, mesh=mesh, in_specs=placed, out_specs=P("group", "rep", None, None), check_vma=False
    )
```

```python
from functools import partial

import jax
import jax.numpy as jnp
from jax import lax
from jax.experimental import pallas as pl
from jax.experimental.pallas import tpu as pltpu
from jax.sharding import PartitionSpec as P


TILE = 128
PER_COL = 2
LEARNING_RATE = 0.1
NX, NY, NC = 4, 4, 2

VMEM = pl.BlockSpec(memory_space=pltpu.VMEM)
HBM = pl.BlockSpec(memory_space=pltpu.HBM)


def place(x, y, c):
    return (x % NX) * NY * NC + (y % NY) * NC + c


PLACES = [(x, y, c) for x in range(NX) for y in range(NY) for c in range(NC)]
X_GROUPS = [[place(x, y, c) for x in range(NX)] for y in range(NY) for c in range(NC)]
Y_GROUPS = [[place(x, y, c) for y in range(NY)] for x in range(NX) for c in range(NC)]


def shift_x(value, by):
    return lax.ppermute(value, "rep", [(place(x, y, c), place(x + by, y, c)) for x, y, c in PLACES])


def swap_cores(value):
    return lax.ppermute(value, "rep", [(place(x, y, c), place(x, y, 1 - c)) for x, y, c in PLACES])


def partner(value, bit):
    return lax.ppermute(value, "group", [(i, i ^ 1 << bit) for i in range(lax.axis_size("group"))])


def exchange(value, groups):
    return lax.all_to_all(value, "rep", 0, 0, tiled=True, axis_index_groups=groups)


def averaged(value, bit):
    return 0.5 * (value + partner(value, bit))


def in_hbm(value):
    return pltpu.with_memory_space_constraint(value, pltpu.HBM)


def round_kernel(gate_ref, up_ref, out_ref, gate_buf, up_buf, sems):
    loads = [
        pltpu.make_async_copy(gate_ref, gate_buf, sems.at[0]),
        pltpu.make_async_copy(up_ref, up_buf, sems.at[1]),
    ]
    for load in loads:
        load.start()
    for number, (load, buf) in enumerate(zip(loads, (gate_buf, up_buf))):
        load.wait()
        low = buf[...].astype(jnp.bfloat16)
        for i in range(NY):
            out_ref[i, number] = low


def rounded(gate, up):
    return pl.pallas_call(
        round_kernel,
        out_shape=jax.ShapeDtypeStruct((NY, 2, *gate.shape), jnp.bfloat16),
        in_specs=[HBM] * 2,
        out_specs=VMEM,
        scratch_shapes=[pltpu.VMEM(gate.shape, jnp.float32)] * 2 + [pltpu.SemaphoreType.DMA((2,))],
        compiler_params=pltpu.CompilerParams(vmem_limit_bytes=4 * 1024 * 1024),
        name="rounded",
    )(in_hbm(gate), in_hbm(up))


def split_kernel(tok_ref, cot_ref, send_ref, mine_ref, sems):
    core = lax.axis_index("rep") % NC
    blocks, hidden = tok_ref.shape[1] // TILE, cot_ref.shape[1] // TILE // NC
    copies = []
    for i in range(blocks):
        copies.append((tok_ref.at[:, pl.ds(i * TILE, TILE)], send_ref.at[i]))
    for i in range(hidden):
        mine = pl.multiple_of((NC * i + core) * TILE, TILE)
        other = pl.multiple_of((NC * i + 1 - core) * TILE, TILE)
        copies.append((cot_ref.at[:, pl.ds(other, TILE)], send_ref.at[blocks + i]))
        copies.append((cot_ref.at[:, pl.ds(mine, TILE)], mine_ref.at[i]))
    started = [pltpu.make_async_copy(a, b, sems.at[n]) for n, (a, b) in enumerate(copies)]
    for copy in started:
        copy.start()
    for copy in started:
        copy.wait()


def split(tok, cot):
    rows, width = tok.shape
    blocks, hidden = width // TILE, cot.shape[1] // TILE // NC
    return pl.pallas_call(
        split_kernel,
        out_shape=(
            jax.ShapeDtypeStruct((blocks + hidden, rows, TILE), jnp.bfloat16),
            jax.ShapeDtypeStruct((hidden, rows, TILE), jnp.bfloat16),
        ),
        in_specs=[HBM] * 2,
        out_specs=(VMEM, VMEM),
        scratch_shapes=[pltpu.SemaphoreType.DMA((blocks + 2 * hidden,))],
        compiler_params=pltpu.CompilerParams(vmem_limit_bytes=8 * 1024 * 1024),
        name="split",
    )(in_hbm(tok), in_hbm(cot))


def grad_kernel(offsets, earlier, rows_ref, send_ref, mine_ref, got_ref, *refs):
    if not earlier and offsets == (0,):
        *refs, got_out, sem = refs
        load = pltpu.make_async_copy(got_ref, got_out, sem)
        load.start()
        load.wait()
        got_ref = got_out
    halves, done, out_ref = refs[: 2 * len(offsets)], refs[2 * len(offsets) : -1], refs[-1]
    scaling = (PER_COL * TILE) ** (-0.5)
    blocks = send_ref.shape[0] - mine_ref.shape[0]
    me = lax.axis_index("rep")
    my_x, core = me // (NY * NC), me % NC
    for ref, group in zip(done, earlier):
        for i, offset in enumerate(group):
            out_ref[lax.rem(my_x + offset, NX)] = ref[i]
    for number, offset in enumerate(offsets):
        column = lax.rem(my_x + offset, NX)
        slot = column if earlier else number

        def one(row, weights, column=column, slot=slot):
            at = column * NY + row
            hidden = at * NC + core
            weight = jnp.concatenate([weights[0], weights[1]], axis=-1)
            first, second = rows_ref[0, hidden], rows_ref[1, hidden]
            total = None
            for tok, cot, base in ((send_ref, mine_ref, 0), (got_ref, got_ref, blocks)):
                selected = jnp.concatenate([tok[first], tok[second]], axis=-1)
                both = jnp.dot(selected, weight, preferred_element_type=jnp.float32) * scaling
                gate, up = both[:, :TILE], both[:, TILE:]
                q = jax.nn.sigmoid(gate)
                grad = cot[base + at].astype(jnp.float32) * up * q * (1.0 + gate * (1.0 - q))
                part = lax.dot_general(
                    selected,
                    grad.astype(jnp.bfloat16),
                    (((0,), (0,)), ((), ())),
                    preferred_element_type=jnp.float32,
                )
                total = part if total is None else total + part
            out_ref[slot, row] = (total * scaling).astype(jnp.bfloat16)

        def pair(i, carry, number=number, one=one):
            one(i, halves[2 * number][i])
            one(NY // 2 + i, halves[2 * number + 1][i])
            return carry

        lax.fori_loop(0, NY // 2, pair, 0)


def partial_sums(offsets, earlier, tile_rows, send, mine, got, halves, done=()):
    columns, first = NX if earlier else len(offsets), not earlier and offsets == (0,)
    out_shape = jax.ShapeDtypeStruct((columns, NY, PER_COL * TILE, TILE), jnp.bfloat16)
    return pl.pallas_call(
        partial(grad_kernel, offsets, earlier),
        out_shape=(out_shape, jax.ShapeDtypeStruct(got.shape, got.dtype)) if first else out_shape,
        in_specs=[pl.BlockSpec(memory_space=pltpu.SMEM), VMEM, VMEM, HBM if first else VMEM]
        + [VMEM] * (len(halves) + len(done)),
        out_specs=(VMEM, VMEM) if first else VMEM,
        scratch_shapes=[pltpu.SemaphoreType.DMA] if first else [],
        compiler_params=pltpu.CompilerParams(vmem_limit_bytes=16 * 1024 * 1024),
    )(tile_rows, send, mine, in_hbm(got) if first else got, *halves, *done)


def body(tokens, cotangent, gate_weight, up_weight, tile_rows, step):
    master = gate_weight[0, 0]
    copies = rounded(master, up_weight[0, 0])
    own = exchange(copies, Y_GROUPS)
    low, high = own[: NY // 2], own[NY // 2 :]
    send, mine = split(tokens[0], cotangent[0])
    got = swap_cores(send)
    left_low = shift_x(low, 1)
    right_high = shift_x(high, -1)
    left_high = shift_x(high, 1)
    right_low = shift_x(low, -1)
    far_low = shift_x(left_low, 1)
    far_high = shift_x(right_high, -1)
    sums = partial(partial_sums, tile_rows=tile_rows.T, send=send, mine=mine)
    part0, got = sums((0,), (), got=got, halves=(low, high))
    part1 = sums((3, 1), (), got=got, halves=(left_low, left_high, right_low, right_high))
    part = sums((2,), ((0,), (3, 1)), got=got, halves=(far_low, far_high), done=(part0, part1))
    got = exchange(part, X_GROUPS)
    column = jnp.sum(got.astype(jnp.float32), axis=0).astype(jnp.bfloat16)
    got = exchange(column, Y_GROUPS)
    total = jnp.sum(got.astype(jnp.float32), axis=0)
    stepped = lax.optimization_barrier(master - LEARNING_RATE * total)
    levels = lax.axis_size("group").bit_length() - 1
    branches = [partial(averaged, bit=number) for number in range(levels)]
    return lax.switch(step[0] % levels, branches, stepped)[None, None]


def solution(mesh):
    placed = (
        P("group", "rep", None),
        P("group", "rep", None),
        P("group", "rep", None, None),
        P("group", "rep", None, None),
        P(),
        P(),
    )
    return jax.shard_map(
        body, mesh=mesh, in_specs=placed, out_specs=P("group", "rep", None, None), check_vma=False
    )
```
